512 devices in a mesh: mp: 8 (over z_lo, core), feat: 64 (over x, z_hi, y).
Axes of the slice: x: 4, y: 4, z: 16 (z_hi: 4, z_lo: 4; z = z_hi * 4 + z_lo), core: 2. Of those that a mesh axis runs over, the one named last changes fastest.
Arguments:
- target_ids: int32 [16], replicated, may hold values from 0 to 127999
- target_pos: int32 [16], replicated, may hold values from 24 to 47
- unembed: bfloat16 [128000, 2304], P(('mp', 'feat')), may hold values from -6 to 6
- attn_weights: float32 [8, 16, 48, 48], P('mp'), may hold values from 0.02 to 1
- inv_rms: float32 [16, 48], replicated, may hold values from 0.5 to 2
- norm_gain: float32 [2304], replicated, may hold values from 0.1 to 1.9
- w_value: bfloat16 [4, 2304, 256], P(None, 'mp'), may hold values from -0.125 to 0.125
- w_out: bfloat16 [8, 256, 2304], P('mp'), may hold values from -0.375 to 0.375
- decoder: bfloat16 [2, 98304, 2304], P(None, ('mp', 'feat')), may hold values from -0.125 to 0.125
- activation: bfloat16 [16, 48, 98304], P(None, None, ('mp', 'feat')), may hold values from 0.5 to 4
- active: int32 [16, 48, 98304], P(None, None, ('mp', 'feat')), may hold values 0 or 1
Outputs:
- attribution: float32 [16, 48, 98304], P(None, None, ('mp', 'feat'))
The draws below stay inside these ranges and needn't reach their ends.
All inputs are finite; a program needn't handle non-finite values. No bound on the sum of `active` on one device may be relied on, other than what follows from the above.
Results may differ from the reference program's by a relative error of at most 0.0035.
Values may be sent and summed in bfloat16 or wider, within the bound.
No kernel may reach another device: no remote copies, remote signals or barrier semaphores. Data moves between devices by JAX's collectives and lax.ppermute only.
A program may use at most 64 MiB of HBM per device.

```python
import math
import jax
import jax.numpy as jnp
from jax import lax

D = 2304
HEADS = 8
KV = 4
HD = 256
FEATS = 98304
VOCAB = 128000
REACH = 2
TARGETS = 16
POS = 48


def set_ends(values, rng, least, largest):
    index_at = [jax.random.randint(jax.random.fold_in(rng, axis), (), 0, length) for axis, length in enumerate(values.shape)]
    widest = values.shape.index(max(values.shape))
    beside = index_at[:widest] + [(index_at[widest] + 1) % values.shape[widest]] + index_at[widest + 1:]
    return values.at[tuple(index_at)].set(least).at[tuple(beside)].set(largest)


def block_scale(key, extent, shards, least, largest):
    loudness, own = 1.0, jax.random.fold_in(key, 6)
    for dim, parts in shards:
        steps = jnp.exp(jax.random.uniform(jax.random.fold_in(own, dim), (parts,), jnp.float32, least / len(shards), largest / len(shards)))
        loudness = loudness * jnp.repeat(steps, extent[dim] // parts).reshape([-1 if axis == dim else 1 for axis in range(len(extent))])
    return loudness


def normal_values(key, shape, deviation, limit, shards=(), kind=jnp.bfloat16):
    entries = deviation * jax.random.normal(key, shape, jnp.float32)
    if shards:
        entries = entries * block_scale(key, shape, shards, -0.22, 0.18)
    return jnp.clip(entries, -limit, limit).astype(kind)


def setup_inputs(seed: int = 0) -> dict:
    seeds = jax.random.split(jax.random.key(seed), 12)
    target_ids = set_ends(jax.random.randint(seeds[0], (TARGETS,), 0, VOCAB), jax.random.fold_in(seeds[0], 1), 0, VOCAB - 1).astype(jnp.int32)
    target_pos = set_ends(jax.random.randint(seeds[1], (TARGETS,), POS // 2, POS), jax.random.fold_in(seeds[1], 1), POS // 2, POS - 1).astype(jnp.int32)
    unembed = normal_values(seeds[2], (VOCAB, D), 1.0, 6.0, ((0, 512),))
    attn_weights = jnp.clip(jnp.exp(math.log(1.0) - 3.912023 * jax.random.uniform(seeds[3], (HEADS, TARGETS, POS, POS), jnp.float32) ** block_scale(seeds[3], (HEADS, TARGETS, POS, POS), ((0, 8),), -0.2, 0.2)), 0.02, 1.0)
    inv_rms = jnp.clip(jnp.exp(jax.random.uniform(seeds[4], (TARGETS, POS), jnp.float32, math.log(0.5), math.log(2.0))), 0.5, 2.0)
    norm_gain = jnp.clip(1.0 + 0.18 * jax.random.normal(seeds[5], (D,), jnp.float32), 0.1, 1.9)
    w_value = normal_values(seeds[6], (KV, D, HD), D ** -0.5, 0.125, ((1, 8),))
    w_out = normal_values(seeds[7], (HEADS, HD, D), HD ** -0.5, 0.375, ((0, 8),))
    decoder = normal_values(seeds[8], (REACH, FEATS, D), D ** -0.5, 0.125, ((1, 512),))
    activation = jnp.clip(jnp.exp(math.log(4.0) - 2.0794415 * jax.random.uniform(seeds[9], (TARGETS, POS, FEATS), jnp.float32) ** block_scale(seeds[9], (TARGETS, POS, FEATS), ((2, 512),), -0.2, 0.2)), 0.5, 4.0).astype(jnp.bfloat16)
    active = set_ends((jax.random.randint(seeds[10], (TARGETS, POS, FEATS), 0, 4) < 1).astype(jnp.int32), jax.random.fold_in(seeds[10], 1), 0, 1)
    return {"target_ids": target_ids, "target_pos": target_pos, "unembed": unembed, "attn_weights": attn_weights, "inv_rms": inv_rms, "norm_gain": norm_gain, "w_value": w_value, "w_out": w_out, "decoder": decoder, "activation": activation, "active": active}


def reference(target_ids, target_pos, unembed, attn_weights, inv_rms, norm_gain, w_value, w_out, decoder, activation, active):
    row_count = TARGETS * POS
    direction = jnp.take(unembed, target_ids, axis=0).astype(jnp.float32)
    placing = (jnp.arange(POS, dtype=jnp.int32)[None, :] == target_pos[:, None]).astype(jnp.float32)
    upper = (placing[:, :, None] * direction[:, None, :]).reshape(row_count, D)
    lowered_top = upper.astype(jnp.bfloat16)
    index_pos = jnp.arange(POS, dtype=jnp.int32)
    causal = (index_pos[:, None] >= index_pos[None, :]).astype(jnp.float32)
    weights = attn_weights * causal
    pattern = weights / jnp.sum(weights, axis=-1, keepdims=True)
    group_size = HEADS // KV
    lowered_wide = lowered_top.astype(jnp.float32).reshape(TARGETS, POS, D)
    heads_sum = jnp.zeros((row_count, D), jnp.float32)
    for head_index in range(HEADS):
        mixed = jnp.einsum("gts,gtd->gsd", pattern[head_index], lowered_wide, precision=lax.Precision.HIGHEST)
        mixed = mixed.reshape(row_count, D).astype(jnp.bfloat16)
        spread = jnp.dot(mixed, w_out[head_index].T, preferred_element_type=jnp.float32).astype(jnp.bfloat16)
        heads_sum = heads_sum + jnp.dot(spread, w_value[head_index // group_size].T, preferred_element_type=jnp.float32)
    below = upper + inv_rms.reshape(row_count, 1) * norm_gain[None, :] * heads_sum
    lowered_bottom = below.astype(jnp.bfloat16)
    scores = jnp.dot(lowered_bottom, decoder[0].T, preferred_element_type=jnp.float32)
    scores = scores + jnp.dot(lowered_top, decoder[1].T, preferred_element_type=jnp.float32)
    attribution = activation.astype(jnp.float32).reshape(row_count, FEATS) * active.reshape(row_count, FEATS).astype(jnp.float32) * scores
    return attribution.reshape(TARGETS, POS, FEATS)
```

```python
import jax
import jax.numpy as jnp
from jax import lax
from jax.sharding import Mesh, PartitionSpec as P

MP = ("zl", "core")
FEAT = ("x", "zh", "y")
ALL = MP + FEAT


def spread_out(block, axes):
    members = lax.axis_size(axes)
    return lax.all_to_all(jnp.broadcast_to(block[None], (members,) + block.shape), axes, 0, 0)


def on_device(
    target_ids,
    target_pos,
    unembed,
    attn_weights,
    inv_rms,
    norm_gain,
    w_value,
    w_out,
    decoder,
    activation,
    active,
):
    vocab_rows, width = unembed.shape
    targets = target_ids.shape[0]
    positions = inv_rms.shape[1]
    kv_heads = w_value.shape[0]
    head_size = w_out.shape[1]
    heads = w_out.shape[0] * lax.axis_size(MP)
    f32 = jnp.float32
    bf16 = jnp.bfloat16

    value_all = lax.all_gather(w_value, MP, axis=1, tiled=True)

    first_row = lax.axis_index(ALL) * vocab_rows
    picker = (
        target_ids[:, None] == first_row + jnp.arange(vocab_rows, dtype=jnp.int32)[None, :]
    ).astype(bf16)
    found = jnp.dot(picker, unembed, preferred_element_type=f32).astype(bf16)
    parts = lax.all_to_all(found, ("x", "y"), 0, 0, tiled=True)
    row = jnp.sum(parts.astype(f32), axis=0).astype(bf16)
    row = jnp.sum(spread_out(row, ("zl", "zh")).astype(f32), axis=0).astype(bf16)
    pairs = spread_out(row, ("x", "y", "core"))
    direction = jnp.sum(pairs.astype(f32).reshape(targets, 2, width), axis=1).astype(bf16)

    key = jnp.arange(positions, dtype=jnp.int32)
    at_target = (key[None, :] == target_pos[:, None]).astype(f32)
    weight_row = jnp.sum(attn_weights[0] * at_target[:, :, None], axis=1)
    weight_row = jnp.where(key[None, :] <= target_pos[:, None], weight_row, 0.0)
    pattern = weight_row / jnp.sum(weight_row, axis=-1, keepdims=True)
    gradient = jnp.einsum("gd,kd->gk", direction, w_out[0], preferred_element_type=f32)
    message = jnp.concatenate(
        [gradient, pattern * inv_rms, jnp.zeros((targets, 128 - positions), f32)], axis=1
    )
    by_head = spread_out(message, MP)
    gradients = by_head[:, :, :head_size].reshape(kv_heads, heads // kv_heads * targets, head_size)
    scale = by_head[:, :, head_size : head_size + positions]

    lowered = jnp.einsum(
        "vrk,vck->vrc", gradients.astype(bf16), value_all, preferred_element_type=f32
    )
    lowered = (lowered * norm_gain[None, None, :]).astype(bf16).reshape(heads * targets, width)
    bottom = jnp.einsum(
        "rd,fd->rf",
        jnp.concatenate([lowered, direction], axis=0),
        decoder[0],
        preferred_element_type=f32,
    )
    top = jnp.einsum("rd,fd->rf", direction, decoder[1], preferred_element_type=f32)
    features = decoder.shape[1]
    per_head = bottom[: heads * targets].reshape(heads, targets, features)
    own = bottom[heads * targets :] + top
    scores = at_target[:, :, None] * own[:, None, :]
    for h in range(heads):
        scores = scores + scale[h][:, :, None] * per_head[h][:, None, :]
    return activation.astype(f32) * active.astype(f32) * scores


def solution(mesh):
    mesh = Mesh(mesh.devices.reshape(4, 2, 4, 4, 4), ALL)
    in_specs = (
        P(),
        P(),
        P(ALL, None),
        P(MP, None, None, None),
        P(),
        P(),
        P(None, MP, None),
        P(MP, None, None),
        P(None, ALL, None),
        P(None, None, ALL),
        P(None, None, ALL),
    )
    out_specs = P(None, None, ALL)
    return jax.shard_map(
        on_device, mesh=mesh, in_specs=in_specs, out_specs=out_specs, check_vma=False
    )
```

```python
import jax
import jax.numpy as jnp
from jax import lax
from jax.sharding import Mesh, PartitionSpec as P

MP = ("zl", "core")
FEAT = ("x", "zh", "y")
ALL = MP + FEAT


def spread_out(block, axes):
    members = lax.axis_size(axes)
    return lax.all_to_all(jnp.broadcast_to(block[None], (members,) + block.shape), axes, 0, 0)


def on_device(
    target_ids,
    target_pos,
    unembed,
    attn_weights,
    inv_rms,
    norm_gain,
    w_value,
    w_out,
    decoder,
    activation,
    active,
):
    vocab_rows, width = unembed.shape
    targets = target_ids.shape[0]
    positions = inv_rms.shape[1]
    kv_heads = w_value.shape[0]
    heads = w_out.shape[0] * lax.axis_size(MP)
    group_size = heads // kv_heads
    f32 = jnp.float32
    bf16 = jnp.bfloat16

    first_row = lax.axis_index(ALL) * vocab_rows
    wanted = jnp.repeat(target_ids, 2)
    picker = (
        wanted[:, None] == first_row + jnp.arange(vocab_rows, dtype=jnp.int32)[None, :]
    ).astype(bf16)
    found = jnp.dot(picker, unembed, preferred_element_type=f32).astype(bf16)
    parts = lax.all_to_all(found, ("x", "y", "core"), 0, 0, tiled=True)
    row = jnp.sum(parts.astype(f32), axis=0).astype(bf16)
    row = jnp.sum(spread_out(row, ("zl", "zh")).astype(f32), axis=0).astype(bf16)[None]

    target = lax.axis_index(("x", "y"))
    here = lax.dynamic_index_in_dim(target_pos, target, 0)
    key = jnp.arange(positions, dtype=jnp.int32)[None]
    weight_row = lax.dynamic_slice(
        attn_weights, (0, target, here[0], 0), (1, 1, 1, positions)
    ).reshape(1, positions)
    weight_row = jnp.where(key <= here[:, None], weight_row, 0.0)
    scale = weight_row / jnp.sum(weight_row, axis=-1, keepdims=True)
    scale = scale * lax.dynamic_slice_in_dim(inv_rms, target, 1, 0)
    high = scale.astype(bf16)
    low = (scale - high.astype(f32)).astype(bf16)
    gap = jnp.zeros((1, 64 - positions), bf16)
    gradient = jnp.einsum("gd,kd->gk", row, w_out[0], preferred_element_type=f32).astype(bf16)
    message = jnp.concatenate([gradient, high, gap, low, gap], axis=1)
    heard = spread_out(message, MP).reshape(heads, w_out.shape[1] + 128)
    head_size = w_out.shape[1]
    lowered = jnp.einsum(
        "vjk,vck->vjc",
        heard[:, :head_size].reshape(kv_heads, group_size, head_size),
        w_value,
        preferred_element_type=f32,
    )
    columns = w_value.shape[1]
    gain = lax.dynamic_slice_in_dim(norm_gain, lax.axis_index(MP) * columns, columns, 0)
    lowered = (lowered * gain).astype(bf16).reshape(heads, columns)
    blocks = spread_out(lowered, MP)
    lowered = jnp.swapaxes(blocks, 0, 1).reshape(heads, width)
    own_row = jnp.pad(row.reshape(heads, columns), ((0, 0), (0, 384 - columns)))
    by_head = jnp.concatenate([lowered, heard[:, head_size:], own_row], axis=1)
    by_target = spread_out(by_head, ("x", "y"))

    direction = by_target[:, :, width + 128 : width + 128 + columns].reshape(targets, width)

    features = decoder.shape[1]
    own = jnp.einsum("rd,fd->rf", direction, decoder[0], preferred_element_type=f32)
    own = own + jnp.einsum("rd,fd->rf", direction, decoder[1], preferred_element_type=f32)
    per_head = jnp.einsum(
        "rd,fd->rf",
        by_target[:, :, :width].reshape(targets * heads, width),
        decoder[0],
        preferred_element_type=f32,
    ).reshape(targets, heads, features)
    scale = by_target[:, :, width : width + positions].astype(f32)
    scale = scale + by_target[:, :, width + 64 : width + 64 + positions].astype(f32)
    at_target = (key == target_pos[:, None]).astype(f32)
    scores = at_target[:, :, None] * own[:, None, :]
    for h in range(heads):
        scores = scores + scale[:, h, :, None] * per_head[:, h, None, :]
    return activation.astype(f32) * active.astype(f32) * scores


def solution(mesh):
    mesh = Mesh(mesh.devices.reshape(4, 2, 4, 4, 4), ALL)
    in_specs = (
        P(),
        P(),
        P(ALL, None),
        P(MP, None, None, None),
        P(),
        P(),
        P(None, MP, None),
        P(MP, None, None),
        P(None, ALL, None),
        P(None, None, ALL),
        P(None, None, ALL),
    )
    out_specs = P(None, None, ALL)
    return jax.shard_map(
        on_device, mesh=mesh, in_specs=in_specs, out_specs=out_specs, check_vma=False
    )
```

```python
import functools

import jax
import jax.numpy as jnp
from jax import lax
from jax.experimental import pallas as pl
from jax.experimental.pallas import tpu as pltpu
from jax.sharding import Mesh, PartitionSpec as P

MP = ("zl", "core")
FEAT = ("x", "zh", "y")
ALL = MP + FEAT
LANES = 128
F32 = jnp.float32
BF16 = jnp.bfloat16
NT = (((1,), (1,)), ((), ()))
VMEM = pl.BlockSpec(memory_space=pltpu.VMEM)
SMEM = pl.BlockSpec(memory_space=pltpu.SMEM)


def call(body, shapes, in_specs, name):
    return pl.pallas_call(
        body,
        out_shape=shapes,
        in_specs=in_specs,
        out_specs=jax.tree.map(lambda _: VMEM, shapes),
        name=name,
        compiler_params=pltpu.CompilerParams(vmem_limit_bytes=32 * 1024 * 1024),
    )


def shape(dims, kind):
    return jax.ShapeDtypeStruct(dims, kind)


def pick_rows(ids, first, unembed, out):
    targets = ids.shape[0]
    rows, width = unembed.shape
    index = lax.broadcasted_iota(jnp.int32, (targets, rows), 0)
    wanted = jnp.zeros((targets, rows), jnp.int32)
    for g in range(targets):
        wanted = jnp.where(index == g, ids[g] - first[0], wanted)
    picker = (wanted == lax.broadcasted_iota(jnp.int32, (targets, rows), 1)).astype(BF16)
    found = jnp.dot(picker, unembed[...], preferred_element_type=F32)
    for g in range(targets):
        row = jnp.concatenate(
            [found[g : g + 1, k * LANES : (k + 1) * LANES] for k in range(width // LANES)], axis=0
        ).astype(BF16)
        out[2 * g] = row
        out[2 * g + 1] = row


def total(parts):
    value = parts[0].astype(F32)
    for i in range(1, parts.shape[0]):
        value = value + parts[i].astype(F32)
    return value


def sum_and_repeat(parts, out):
    row = total(parts).astype(BF16)
    for i in range(out.shape[0]):
        out[i] = row


def query_gradient(position, target, parts, w_out, attn, inv_rms, row_out, out):
    row = total(parts)
    row_out[...] = row.astype(BF16)
    flat = jnp.concatenate([row[k : k + 1, :] for k in range(row.shape[0])], axis=1).astype(BF16)
    gradient = lax.dot_general(flat, w_out[...], NT, preferred_element_type=F32)
    here = position[target[0]]
    weights = attn[target[0], pl.ds(here, 1), :]
    key = lax.broadcasted_iota(jnp.int32, weights.shape, 1)
    weights = jnp.where(key <= here, weights, 0.0)
    scale = weights / jnp.sum(weights, axis=1, keepdims=True)
    scale = scale * inv_rms[pl.ds(target[0], 1), :]
    positions = weights.shape[1]
    for i in range(out.shape[0]):
        for k in range(gradient.shape[1] // LANES):
            out[i, k : k + 1, :] = gradient[:, k * LANES : (k + 1) * LANES]
        out[i, 2:3, 0:positions] = scale
        out[i, 2:3, positions:] = jnp.zeros((1, LANES - positions), F32)


def lower_block(heard, w_value, gain, out):
    heads = heard.shape[0]
    kv_heads, columns, _ = w_value.shape
    gradient = jnp.concatenate([heard[:, 0, :], heard[:, 1, :]], axis=1).astype(BF16)
    head = lax.broadcasted_iota(jnp.int32, (heads, columns), 0)
    lowered = jnp.zeros((heads, columns), F32)
    for v in range(kv_heads):
        value = lax.dot_general(gradient, w_value[v], NT, preferred_element_type=F32)
        lowered = jnp.where(head // (heads // kv_heads) == v, value, lowered)
    lowered = (lowered * gain[...]).astype(BF16)
    for i in range(out.shape[0]):
        out[i] = lowered


def build_message(blocks, heard, row, out):
    heads = heard.shape[0]
    members = blocks.shape[0]
    width = members * blocks.shape[2]
    lowered = jnp.concatenate([blocks[i].astype(F32) for i in range(members)], axis=1)
    scale = heard[:, 2, :]
    high = scale.astype(BF16).astype(F32)
    low = scale - high
    both = (high + pltpu.roll(low, LANES // 2, 1)).astype(BF16)
    lowered = lowered.astype(BF16)
    rows = row[...].astype(F32)
    count = rows.shape[0]
    for i in range(out.shape[0]):
        out[i, :, 0:width] = lowered
        out[i, :, width : width + LANES] = both
    for j in range(-(-count // heads)):
        some = rows[j * heads : min((j + 1) * heads, count)]
        if some.shape[0] < heads:
            some = jnp.concatenate([some, jnp.zeros((heads - some.shape[0], LANES), F32)], axis=0)
        some = some.astype(BF16)
        start = width + (j + 1) * LANES
        for i in range(out.shape[0]):
            out[i, :, start : start + LANES] = some


def score(position, message, decoder, activation, active, out):
    targets, heads, _ = message.shape
    _, features, width = decoder.shape
    positions = activation.shape[1]
    count = width // LANES
    chunks = message[:, :, width + LANES :].astype(F32)
    direction = jnp.concatenate(
        [
            chunks[:, k % heads, (k // heads) * LANES : (k // heads + 1) * LANES]
            for k in range(count)
        ],
        axis=1,
    ).astype(BF16)
    own = lax.dot_general(direction, decoder[0], NT, preferred_element_type=F32)
    own = own + lax.dot_general(direction, decoder[1], NT, preferred_element_type=F32)
    lowered = message[:, :, 0:width].reshape(targets * heads, width)
    per_head = lax.dot_general(lowered, decoder[0], NT, preferred_element_type=F32)
    scale = message[:, :, width : width + LANES].astype(F32)
    key = lax.broadcasted_iota(jnp.int32, (heads, LANES), 1)
    first = lax.broadcasted_iota(jnp.int32, (heads, LANES), 0) == 0
    spare = jnp.zeros((heads - 1, features), F32)
    for g in range(targets):
        both = scale[g] + pltpu.roll(scale[g], LANES // 2, 1)
        here = jnp.where(first & (key == position[g]), 1.0, 0.0)
        left = jnp.concatenate([both, here], axis=0)[:, 0:positions]
        right = jnp.concatenate(
            [per_head[g * heads : (g + 1) * heads], own[g : g + 1], spare], axis=0
        )
        scores = lax.dot_general(
            left,
            right,
            (((0,), (0,)), ((), ())),
            precision=lax.Precision.HIGHEST,
            preferred_element_type=F32,
        )
        out[g] = activation[g].astype(F32) * active[g].astype(F32) * scores


def on_device(
    target_ids,
    target_pos,
    unembed,
    attn_weights,
    inv_rms,
    norm_gain,
    w_value,
    w_out,
    decoder,
    activation,
    active,
):
    vocab_rows, width = unembed.shape
    targets = target_ids.shape[0]
    tiles = width // LANES
    columns = w_value.shape[1]
    heads = lax.axis_size(MP)
    first_row = (lax.axis_index(ALL) * vocab_rows).reshape(1)
    target = lax.axis_index(("x", "y")).reshape(1)
    gain = lax.dynamic_slice_in_dim(norm_gain, lax.axis_index(MP) * columns, columns, 0)[None]

    found = call(
        pick_rows, shape((2 * targets, tiles, LANES), BF16), [SMEM, SMEM, VMEM], "pick_rows"
    )(target_ids, first_row, unembed)
    parts = lax.all_to_all(found, ("x", "y", "core"), 0, 0, tiled=True)
    ring = lax.axis_size(("zl", "zh"))
    parts = call(sum_and_repeat, shape((ring, tiles, LANES), BF16), [VMEM], "sum_and_repeat")(parts)
    parts = lax.all_to_all(parts, ("zl", "zh"), 0, 0, tiled=True)
    row, asked = call(
        query_gradient,
        (shape((tiles, LANES), BF16), shape((heads, 8, LANES), F32)),
        [SMEM, SMEM, VMEM, VMEM, VMEM, VMEM],
        "query_gradient",
    )(target_pos, target, parts, w_out[0], attn_weights[0], inv_rms)
    heard = lax.all_to_all(asked, MP, 0, 0, tiled=True)
    blocks = call(
        lower_block, shape((heads, heads, columns), BF16), [VMEM, VMEM, VMEM], "lower_block"
    )(heard, w_value, gain)
    blocks = lax.all_to_all(blocks, MP, 0, 0, tiled=True)
    length = width + LANES + -(-tiles // heads) * LANES
    message = call(
        build_message, shape((targets, heads, length), BF16), [VMEM, VMEM, VMEM], "build_message"
    )(blocks, heard, row)
    message = lax.all_to_all(message, ("x", "y"), 0, 0, tiled=True)
    return call(score, shape(activation.shape, F32), [SMEM, VMEM, VMEM, VMEM, VMEM], "score")(
        target_pos, message, decoder, activation, active
    )


def solution(mesh):
    mesh = Mesh(mesh.devices.reshape(4, 2, 4, 4, 4), ALL)
    in_specs = (
        P(),
        P(),
        P(ALL, None),
        P(MP, None, None, None),
        P(),
        P(),
        P(None, MP, None),
        P(MP, None, None),
        P(None, ALL, None),
        P(None, None, ALL),
        P(None, None, ALL),
    )
    out_specs = P(None, None, ALL)
    return jax.shard_map(
        on_device, mesh=mesh, in_specs=in_specs, out_specs=out_specs, check_vma=False
    )
```

```python
import jax
import jax.numpy as jnp
from jax import lax
from jax.experimental import pallas as pl
from jax.experimental.pallas import tpu as pltpu
from jax.sharding import Mesh, PartitionSpec as P

MP = ("zl", "core")
FEAT = ("x", "zh", "y")
ALL = MP + FEAT
LANES = 128
F32 = jnp.float32
BF16 = jnp.bfloat16
NT = (((1,), (1,)), ((), ()))
VMEM = pl.BlockSpec(memory_space=pltpu.VMEM)
SMEM = pl.BlockSpec(memory_space=pltpu.SMEM)
HBM = pl.BlockSpec(memory_space=pltpu.HBM)


def call(body, shapes, in_specs, name):
    return pl.pallas_call(
        body,
        out_shape=shapes,
        in_specs=in_specs,
        out_specs=jax.tree.map(lambda _: VMEM, shapes),
        name=name,
        compiler_params=pltpu.CompilerParams(vmem_limit_bytes=32 * 1024 * 1024),
    )


def shape(dims, kind):
    return jax.ShapeDtypeStruct(dims, kind)


def pick_rows(first, ids_hbm, unembed_hbm, out, ids, unembed, sems):
    ids_copy = pltpu.make_async_copy(ids_hbm, ids, sems.at[0])
    rows_copy = pltpu.make_async_copy(unembed_hbm, unembed, sems.at[1])
    ids_copy.start()
    rows_copy.start()
    targets = ids.shape[0]
    rows, width = unembed.shape
    index = lax.broadcasted_iota(jnp.int32, (targets, rows), 0)
    wanted = jnp.zeros((targets, rows), jnp.int32)
    ids_copy.wait()
    for g in range(targets):
        wanted = jnp.where(index == g, ids[g] - first[0], wanted)
    picker = (wanted == lax.broadcasted_iota(jnp.int32, (targets, rows), 1)).astype(BF16)
    rows_copy.wait()
    found = jnp.dot(picker, unembed[...], preferred_element_type=F32)
    half = width // 2
    for g in range(targets):
        row = jnp.concatenate([found[g : g + 1, :half], found[g : g + 1, half:]], axis=0)
        row = row.astype(BF16)
        out[2 * g] = row
        out[2 * g + 1] = row


def total(parts):
    value = parts[0].astype(F32)
    for i in range(1, parts.shape[0]):
        value = value + parts[i].astype(F32)
    return value


def sum_and_repeat(parts, out):
    row = total(parts).astype(BF16)
    for i in range(out.shape[0]):
        out[i] = row


def query_gradient(position, target, parts, w_out, attn, inv_rms, row_out, out):
    row = total(parts)
    row_out[...] = row
    flat = jnp.concatenate([row[0:1], row[1:2]], axis=1).astype(BF16)
    gradient = lax.dot_general(flat, w_out[...], NT, preferred_element_type=F32)
    here = position[target[0]]
    weights = attn[target[0], pl.ds(here, 1), :]
    key = lax.broadcasted_iota(jnp.int32, weights.shape, 1)
    weights = jnp.where(key <= here, weights, 0.0)
    scale = weights / jnp.sum(weights, axis=1, keepdims=True)
    scale = scale * inv_rms[pl.ds(target[0], 1), :]
    positions = weights.shape[1]
    for i in range(out.shape[0]):
        for k in range(gradient.shape[1] // LANES):
            out[i, k : k + 1, :] = gradient[:, k * LANES : (k + 1) * LANES]
        out[i, 2:3, 0:positions] = scale
        out[i, 2:3, positions:] = jnp.zeros((1, LANES - positions), F32)


def lower_block(block, heard, w_value, gain, out):
    heads = heard.shape[0]
    kv_heads, columns, _ = w_value.shape
    gradient = jnp.concatenate([heard[:, 0, :], heard[:, 1, :]], axis=1).astype(BF16)
    head = lax.broadcasted_iota(jnp.int32, (heads, columns), 0)
    lowered = jnp.zeros((heads, columns), F32)
    for v in range(kv_heads):
        value = lax.dot_general(gradient, w_value[v], NT, preferred_element_type=F32)
        lowered = jnp.where(head // (heads // kv_heads) == v, value, lowered)
    own_gain = jnp.zeros((1, columns), F32)
    for i in range(heads):
        part = gain[:, i * columns : (i + 1) * columns]
        own_gain = jnp.where(block[0] == i, part, own_gain)
    lowered = (lowered * own_gain).astype(BF16)
    for i in range(out.shape[0]):
        out[i] = lowered


def build_message(blocks, heard, row, out):
    heads = heard.shape[0]
    members = blocks.shape[0]
    width = members * blocks.shape[2]
    lowered = jnp.concatenate([blocks[i].astype(F32) for i in range(members)], axis=1)
    scale = heard[:, 2, :]
    high = scale.astype(BF16).astype(F32)
    low = scale - high
    both = (high + pltpu.roll(low, LANES // 2, 1)).astype(BF16)
    lowered = lowered.astype(BF16)
    half = row.shape[1] // LANES
    rows = [
        row[k // half : k // half + 1, (k % half) * LANES : (k % half + 1) * LANES]
        for k in range(2 * half)
    ]
    rows = rows + [jnp.zeros((1, LANES), F32)] * (-len(rows) % heads)
    for i in range(out.shape[0]):
        out[i, :, 0:width] = lowered
        out[i, :, width : width + LANES] = both
    for j in range(len(rows) // heads):
        some = jnp.concatenate(rows[j * heads : (j + 1) * heads], axis=0).astype(BF16)
        start = width + (j + 1) * LANES
        for i in range(out.shape[0]):
            out[i, :, start : start + LANES] = some


def score(position, message, decoder, activation, active, out):
    targets, heads, _ = message.shape
    _, features, width = decoder.shape
    positions = activation.shape[1]
    count = width // LANES
    chunks = message[:, :, width + LANES :].astype(F32)
    direction = jnp.concatenate(
        [
            chunks[:, k % heads, (k // heads) * LANES : (k // heads + 1) * LANES]
            for k in range(count)
        ],
        axis=1,
    ).astype(BF16)
    lowered = message[:, :, 0:width].reshape(targets * heads, width)
    both = jnp.concatenate([lowered, direction], axis=0)
    bottom = lax.dot_general(both, decoder[0], NT, preferred_element_type=F32)
    top = lax.dot_general(direction, decoder[1], NT, preferred_element_type=F32)
    per_head = bottom[0 : targets * heads]
    own = bottom[targets * heads :] + top
    per_head_high = per_head.astype(BF16).astype(F32)
    per_head_low = per_head - per_head_high
    own_high = own.astype(BF16).astype(F32)
    own_low = own - own_high
    scale = message[:, :, width : width + LANES].astype(F32)
    key = lax.broadcasted_iota(jnp.int32, (heads, LANES), 1)
    below_two = lax.broadcasted_iota(jnp.int32, (heads, LANES), 0) < 2
    spare = jnp.zeros((heads - 2, features), F32)
    for g in range(targets):
        high = scale[g]
        low = pltpu.roll(high, LANES // 2, 1)
        here = jnp.where(below_two & (key == position[g]), 1.0, 0.0)
        mine = slice(g * heads, (g + 1) * heads)
        left = jnp.concatenate([high, low, high, here], axis=0)[:, 0:positions].astype(BF16)
        right = jnp.concatenate(
            [
                per_head_high[mine],
                per_head_high[mine],
                per_head_low[mine],
                own_high[g : g + 1],
                own_low[g : g + 1],
                spare,
            ],
            axis=0,
        ).astype(BF16)
        scores = lax.dot_general(
            left, right, (((0,), (0,)), ((), ())), preferred_element_type=F32
        )
        out[g] = activation[g].astype(F32) * active[g].astype(F32) * scores


def on_device(
    target_ids,
    target_pos,
    unembed,
    attn_weights,
    inv_rms,
    norm_gain,
    w_value,
    w_out,
    decoder,
    activation,
    active,
):
    vocab_rows, width = unembed.shape
    targets = target_ids.shape[0]
    tiles = width // LANES
    columns = w_value.shape[1]
    heads = lax.axis_size(MP)
    first_row = (lax.axis_index(ALL) * vocab_rows).reshape(1)
    target = lax.axis_index(("x", "y")).reshape(1)
    block = lax.axis_index(MP).reshape(1)

    found = pl.pallas_call(
        pick_rows,
        out_shape=shape((2 * targets, 2, width // 2), BF16),
        in_specs=[SMEM, HBM, HBM],
        out_specs=VMEM,
        scratch_shapes=[
            pltpu.SMEM((targets,), jnp.int32),
            pltpu.VMEM((vocab_rows, width), BF16),
            pltpu.SemaphoreType.DMA((2,)),
        ],
        name="pick_rows",
        compiler_params=pltpu.CompilerParams(vmem_limit_bytes=32 * 1024 * 1024),
    )(
        first_row,
        pltpu.with_memory_space_constraint(target_ids, pltpu.HBM),
        pltpu.with_memory_space_constraint(unembed, pltpu.HBM),
    )
    parts = lax.all_to_all(found, ("x", "y", "core"), 0, 0, tiled=True)
    ring = lax.axis_size(("zl", "zh"))
    parts = call(
        sum_and_repeat, shape((ring, 2, width // 2), BF16), [VMEM], "sum_and_repeat"
    )(parts)
    parts = lax.all_to_all(parts, ("zl", "zh"), 0, 0, tiled=True)
    row, asked = call(
        query_gradient,
        (shape((2, width // 2), F32), shape((heads, 8, LANES), F32)),
        [SMEM, SMEM, VMEM, VMEM, VMEM, VMEM],
        "query_gradient",
    )(target_pos, target, parts, w_out[0], attn_weights[0], inv_rms)
    heard = lax.all_to_all(asked, MP, 0, 0, tiled=True)
    blocks = call(
        lower_block,
        shape((heads, heads, columns), BF16),
        [SMEM, VMEM, VMEM, VMEM],
        "lower_block",
    )(block, heard, w_value, norm_gain[None])
    blocks = lax.all_to_all(blocks, MP, 0, 0, tiled=True)
    length = width + LANES + -(-tiles // heads) * LANES
    message = call(
        build_message, shape((targets, heads, length), BF16), [VMEM, VMEM, VMEM], "build_message"
    )(blocks, heard, row)
    message = lax.all_to_all(message, ("x", "y"), 0, 0, tiled=True)
    return call(score, shape(activation.shape, F32), [SMEM, VMEM, VMEM, VMEM, VMEM], "score")(
        target_pos, message, decoder, activation, active
    )


def solution(mesh):
    mesh = Mesh(mesh.devices.reshape(4, 2, 4, 4, 4), ALL)
    in_specs = (
        P(),
        P(),
        P(ALL, None),
        P(MP, None, None, None),
        P(),
        P(),
        P(None, MP, None),
        P(MP, None, None),
        P(None, ALL, None),
        P(None, None, ALL),
        P(None, None, ALL),
    )
    out_specs = P(None, None, ALL)
    return jax.shard_map(
        on_device, mesh=mesh, in_specs=in_specs, out_specs=out_specs, check_vma=False
    )
```

```python
import jax
import jax.numpy as jnp
from jax import lax
from jax.experimental import pallas as pl
from jax.experimental.pallas import tpu as pltpu
from jax.sharding import Mesh, PartitionSpec as P

MP = ("zl", "core")
FEAT = ("x", "zh", "y")
ALL = MP + FEAT
LANES = 128
F32 = jnp.float32
BF16 = jnp.bfloat16
NT = (((1,), (1,)), ((), ()))
VMEM = pl.BlockSpec(memory_space=pltpu.VMEM)
SMEM = pl.BlockSpec(memory_space=pltpu.SMEM)
HBM = pl.BlockSpec(memory_space=pltpu.HBM)


def call(body, shapes, in_specs, name):
    return pl.pallas_call(
        body,
        out_shape=shapes,
        in_specs=in_specs,
        out_specs=jax.tree.map(lambda _: VMEM, shapes),
        name=name,
        compiler_params=pltpu.CompilerParams(vmem_limit_bytes=32 * 1024 * 1024),
    )


def shape(dims, kind):
    return jax.ShapeDtypeStruct(dims, kind)


def share_rows(target, block, found, out):
    del target, block
    half = out.shape[2]
    for g in range(found.shape[0]):
        row = jnp.concatenate([found[g : g + 1, :half], found[g : g + 1, half:]], axis=0)
        row = row.astype(BF16)
        out[2 * g] = row
        out[2 * g + 1] = row


def total(parts):
    value = parts[0].astype(F32)
    for i in range(1, parts.shape[0]):
        value = value + parts[i].astype(F32)
    return value


def sum_and_repeat(parts, out):
    row = total(parts).astype(BF16)
    for i in range(out.shape[0]):
        out[i] = row


def query_gradient(position, target, parts, w_out, attn, inv_rms, row_out, out):
    row = total(parts)
    row_out[...] = row
    flat = jnp.concatenate([row[0:1], row[1:2]], axis=1).astype(BF16)
    gradient = lax.dot_general(flat, w_out[...], NT, preferred_element_type=F32)
    here = position[target[0]]
    weights = attn[target[0], pl.ds(here, 1), :]
    key = lax.broadcasted_iota(jnp.int32, weights.shape, 1)
    weights = jnp.where(key <= here, weights, 0.0)
    scale = weights / jnp.sum(weights, axis=1, keepdims=True)
    scale = scale * inv_rms[pl.ds(target[0], 1), :]
    positions = weights.shape[1]
    for i in range(out.shape[0]):
        for k in range(gradient.shape[1] // LANES):
            out[i, k : k + 1, :] = gradient[:, k * LANES : (k + 1) * LANES]
        out[i, 2:3, 0:positions] = scale
        out[i, 2:3, positions:] = jnp.zeros((1, LANES - positions), F32)


def lower_block(block, heard, w_value, gain, out):
    heads = heard.shape[0]
    kv_heads, columns, _ = w_value.shape
    gradient = jnp.concatenate([heard[:, 0, :], heard[:, 1, :]], axis=1).astype(BF16)
    head = lax.broadcasted_iota(jnp.int32, (heads, columns), 0)
    lowered = jnp.zeros((heads, columns), F32)
    for v in range(kv_heads):
        value = lax.dot_general(gradient, w_value[v], NT, preferred_element_type=F32)
        lowered = jnp.where(head // (heads // kv_heads) == v, value, lowered)
    whole = gain[...].reshape(1, heads * columns)
    own_gain = jnp.zeros((1, columns), F32)
    for i in range(heads):
        part = whole[:, i * columns : (i + 1) * columns]
        own_gain = jnp.where(block[0] == i, part, own_gain)
    lowered = (lowered * own_gain).astype(BF16)
    for i in range(out.shape[0]):
        out[i] = lowered


def build_message(blocks, heard, row, out):
    heads = heard.shape[0]
    members = blocks.shape[0]
    width = members * blocks.shape[2]
    lowered = jnp.concatenate([blocks[i].astype(F32) for i in range(members)], axis=1)
    scale = heard[:, 2, :]
    high = scale.astype(BF16).astype(F32)
    low = scale - high
    both = (high + pltpu.roll(low, LANES // 2, 1)).astype(BF16)
    lowered = lowered.astype(BF16)
    half = row.shape[1] // LANES
    rows = [
        row[k // half : k // half + 1, (k % half) * LANES : (k % half + 1) * LANES]
        for k in range(2 * half)
    ]
    rows = rows + [jnp.zeros((1, LANES), F32)] * (-len(rows) % heads)
    for i in range(out.shape[0]):
        out[i, :, 0:width] = lowered
        out[i, :, width : width + LANES] = both
    for j in range(len(rows) // heads):
        some = jnp.concatenate(rows[j * heads : (j + 1) * heads], axis=0).astype(BF16)
        start = width + (j + 1) * LANES
        for i in range(out.shape[0]):
            out[i, :, start : start + LANES] = some


def score(position, message, decoder, activation, active, out_hbm, out, sems):
    targets, heads, _ = message.shape
    _, features, width = decoder.shape
    positions = activation.shape[1]
    count = width // LANES
    chunks = message[:, :, width + LANES :].astype(F32)
    direction = jnp.concatenate(
        [
            chunks[:, k % heads, (k // heads) * LANES : (k // heads + 1) * LANES]
            for k in range(count)
        ],
        axis=1,
    ).astype(BF16)
    lowered = message[:, :, 0:width].reshape(targets * heads, width)
    both = jnp.concatenate([lowered, direction], axis=0)
    bottom = lax.dot_general(both, decoder[0], NT, preferred_element_type=F32)
    top = lax.dot_general(direction, decoder[1], NT, preferred_element_type=F32)
    per_head = bottom[0 : targets * heads]
    own = bottom[targets * heads :] + top
    per_head_high = per_head.astype(BF16).astype(F32)
    per_head_low = per_head - per_head_high
    own_high = own.astype(BF16).astype(F32)
    own_low = own - own_high
    scale = message[:, :, width : width + LANES].astype(F32)
    key = lax.broadcasted_iota(jnp.int32, (heads, LANES), 1)
    below_two = lax.broadcasted_iota(jnp.int32, (heads, LANES), 0) < 2
    spare = jnp.zeros((heads - 2, features), F32)
    step = targets // 4
    copies = []
    for g in range(targets):
        high = scale[g]
        low = pltpu.roll(high, LANES // 2, 1)
        here = jnp.where(below_two & (key == position[g]), 1.0, 0.0)
        mine = slice(g * heads, (g + 1) * heads)
        left = jnp.concatenate([high, low, high, here], axis=0)[:, 0:positions].astype(BF16)
        right = jnp.concatenate(
            [
                per_head_high[mine],
                per_head_high[mine],
                per_head_low[mine],
                own_high[g : g + 1],
                own_low[g : g + 1],
                spare,
            ],
            axis=0,
        ).astype(BF16)
        scores = lax.dot_general(
            left, right, (((0,), (0,)), ((), ())), preferred_element_type=F32
        )
        out[g] = activation[g].astype(F32) * active[g].astype(F32) * scores
        if (g + 1) % step == 0:
            copies.append(
                pltpu.make_async_copy(
                    out.at[g + 1 - step : g + 1], out_hbm.at[g + 1 - step : g + 1], sems.at[g // step]
                )
            )
            copies[-1].start()
    for copy in copies:
        copy.wait()


def on_device(
    target_ids,
    target_pos,
    unembed,
    attn_weights,
    inv_rms,
    norm_gain,
    w_value,
    w_out,
    decoder,
    activation,
    active,
):
    vocab_rows, width = unembed.shape
    targets = target_ids.shape[0]
    tiles = width // LANES
    columns = w_value.shape[1]
    heads = lax.axis_size(MP)
    first_row = lax.axis_index(ALL) * vocab_rows
    target = lax.axis_index(("x", "y")).reshape(1)
    block = lax.axis_index(MP).reshape(1)

    own = first_row + jnp.arange(vocab_rows, dtype=jnp.int32)
    picker = (target_ids[:, None] == own[None, :]).astype(BF16)
    found = jnp.dot(picker, unembed, preferred_element_type=F32)
    found = call(
        share_rows, shape((2 * targets, 2, width // 2), BF16), [SMEM, SMEM, VMEM], "share_rows"
    )(target, block, found)
    parts = lax.all_to_all(found, ("x", "y", "core"), 0, 0, tiled=True)
    ring = lax.axis_size(("zl", "zh"))
    parts = call(
        sum_and_repeat, shape((ring, 2, width // 2), BF16), [VMEM], "sum_and_repeat"
    )(parts)
    parts = lax.all_to_all(parts, ("zl", "zh"), 0, 0, tiled=True)
    row, asked = call(
        query_gradient,
        (shape((2, width // 2), F32), shape((heads, 8, LANES), F32)),
        [SMEM, SMEM, VMEM, VMEM, VMEM, VMEM],
        "query_gradient",
    )(target_pos, target, parts, w_out[0], attn_weights[0], inv_rms)
    heard = lax.all_to_all(asked, MP, 0, 0, tiled=True)
    blocks = call(
        lower_block,
        shape((heads, heads, columns), BF16),
        [SMEM, VMEM, VMEM, VMEM],
        "lower_block",
    )(block, heard, w_value, norm_gain)
    blocks = lax.all_to_all(blocks, MP, 0, 0, tiled=True)
    length = width + LANES + -(-tiles // heads) * LANES
    message = call(
        build_message, shape((targets, heads, length), BF16), [VMEM, VMEM, VMEM], "build_message"
    )(blocks, heard, row)
    message = lax.all_to_all(message, ("x", "y"), 0, 0, tiled=True)
    return pl.pallas_call(
        score,
        out_shape=shape(activation.shape, F32),
        in_specs=[SMEM, VMEM, VMEM, VMEM, VMEM],
        out_specs=HBM,
        scratch_shapes=[pltpu.VMEM(activation.shape, F32), pltpu.SemaphoreType.DMA((4,))],
        name="score",
        compiler_params=pltpu.CompilerParams(vmem_limit_bytes=32 * 1024 * 1024),
    )(target_pos, message, decoder, activation, active)


def solution(mesh):
    mesh = Mesh(mesh.devices.reshape(4, 2, 4, 4, 4), ALL)
    in_specs = (
        P(),
        P(),
        P(ALL, None),
        P(MP, None, None, None),
        P(),
        P(),
        P(None, MP, None),
        P(MP, None, None),
        P(None, ALL, None),
        P(None, None, ALL),
        P(None, None, ALL),
    )
    out_specs = P(None, None, ALL)
    return jax.shard_map(
        on_device, mesh=mesh, in_specs=in_specs, out_specs=out_specs, check_vma=False
    )
```

```python
import jax
import jax.numpy as jnp
from jax import lax
from jax.experimental import pallas as pl
from jax.experimental.pallas import tpu as pltpu
from jax.sharding import Mesh, PartitionSpec as P

MP = ("zl", "core")
FEAT = ("x", "zh", "y")
ALL = MP + FEAT
LANES = 128
POSITIONS = 48
F32 = jnp.float32
BF16 = jnp.bfloat16
NT = (((1,), (1,)), ((), ()))
VMEM = pl.BlockSpec(memory_space=pltpu.VMEM)
SMEM = pl.BlockSpec(memory_space=pltpu.SMEM)
HBM = pl.BlockSpec(memory_space=pltpu.HBM)


def call(body, shapes, in_specs, name):
    return pl.pallas_call(
        body,
        out_shape=shapes,
        in_specs=in_specs,
        out_specs=jax.tree.map(lambda _: VMEM, shapes),
        name=name,
        compiler_params=pltpu.CompilerParams(vmem_limit_bytes=32 * 1024 * 1024),
    )


def shape(dims, kind):
    return jax.ShapeDtypeStruct(dims, kind)


def share_rows(target, block, found, out):
    del target, block
    half = out.shape[2]
    for g in range(found.shape[0]):
        row = jnp.concatenate([found[g : g + 1, :half], found[g : g + 1, half:]], axis=0)
        row = row.astype(BF16)
        out[2 * g] = row
        out[2 * g + 1] = row


def total(parts):
    value = parts[0].astype(F32)
    for i in range(1, parts.shape[0]):
        value = value + parts[i].astype(F32)
    return value


def sum_and_repeat(parts, out):
    row = total(parts).astype(BF16)
    for i in range(out.shape[0]):
        out[i] = row


def query_gradient(position, target, parts, w_out, attn, inv_rms, row_out, out):
    row = total(parts)
    row_out[...] = row
    flat = jnp.concatenate([row[0:1], row[1:2]], axis=1).astype(BF16)
    gradient = lax.dot_general(flat, w_out[...], NT, preferred_element_type=F32)
    here = position[target[0]]
    weights = attn[target[0], pl.ds(here, 1), :]
    key = lax.broadcasted_iota(jnp.int32, weights.shape, 1)
    weights = jnp.where(key <= here, weights, 0.0)
    scale = weights / jnp.sum(weights, axis=1, keepdims=True)
    scale = scale * inv_rms[pl.ds(target[0], 1), :]
    positions = weights.shape[1]
    for i in range(out.shape[0]):
        for k in range(gradient.shape[1] // LANES):
            out[i, k : k + 1, :] = gradient[:, k * LANES : (k + 1) * LANES]
        out[i, 2:3, 0:positions] = scale
        out[i, 2:3, positions:] = jnp.zeros((1, LANES - positions), F32)


def lower_block(block, heard, w_value, gain, out):
    heads = heard.shape[0]
    kv_heads, columns, _ = w_value.shape
    gradient = jnp.concatenate([heard[:, 0, :], heard[:, 1, :]], axis=1).astype(BF16)
    head = lax.broadcasted_iota(jnp.int32, (heads, columns), 0)
    lowered = jnp.zeros((heads, columns), F32)
    for v in range(kv_heads):
        value = lax.dot_general(gradient, w_value[v], NT, preferred_element_type=F32)
        lowered = jnp.where(head // (heads // kv_heads) == v, value, lowered)
    whole = gain[...].reshape(1, heads * columns)
    own_gain = jnp.zeros((1, columns), F32)
    for i in range(heads):
        part = whole[:, i * columns : (i + 1) * columns]
        own_gain = jnp.where(block[0] == i, part, own_gain)
    lowered = (lowered * own_gain).astype(BF16)
    for i in range(out.shape[0]):
        out[i] = lowered


def build_message(blocks, heard, row, out):
    heads = heard.shape[0]
    members = blocks.shape[0]
    width = members * blocks.shape[2]
    lowered = jnp.concatenate([blocks[i].astype(F32) for i in range(members)], axis=1)
    lowered = lowered.astype(BF16)
    scale = heard[:, 2, 0:POSITIONS]
    high = scale.astype(BF16).astype(F32)
    flat = jnp.concatenate([row[0:1], row[1:2]], axis=1)
    columns = width // heads
    rows = jnp.concatenate(
        [flat[:, i * columns : (i + 1) * columns] for i in range(heads)], axis=0
    )
    tail = jnp.concatenate([high, scale - high, rows], axis=1).astype(BF16)
    for i in range(out.shape[0]):
        out[i, :, 0:width] = lowered
        out[i, :, width:] = tail


def score(position, message, decoder, activation, active, out_hbm, out, sems):
    targets, heads, _ = message.shape
    _, features, width = decoder.shape
    positions = activation.shape[1]
    columns = width // heads
    tail = message[:, :, width:].astype(F32)
    chunks = tail[:, :, 2 * positions : 2 * positions + columns]
    direction = jnp.concatenate([chunks[:, i, :] for i in range(heads)], axis=1).astype(BF16)
    lowered = message[:, :, 0:width].reshape(targets * heads, width)
    both = jnp.concatenate([lowered, direction], axis=0)
    bottom = lax.dot_general(both, decoder[0], NT, preferred_element_type=F32)
    top = lax.dot_general(direction, decoder[1], NT, preferred_element_type=F32)
    per_head = bottom[0 : targets * heads]
    own = bottom[targets * heads :] + top
    per_head_high = per_head.astype(BF16).astype(F32)
    per_head_low = per_head - per_head_high
    own_high = own.astype(BF16).astype(F32)
    own_low = own - own_high
    scale = tail[:, :, 0:LANES]
    key = lax.broadcasted_iota(jnp.int32, (heads, LANES), 1)
    below_two = lax.broadcasted_iota(jnp.int32, (heads, LANES), 0) < 2
    spare = jnp.zeros((heads - 2, features), F32)
    step = targets // 4
    copies = []
    for g in range(targets):
        high = scale[g]
        low = pltpu.roll(high, LANES - positions, 1)
        here = jnp.where(below_two & (key == position[g]), 1.0, 0.0)
        mine = slice(g * heads, (g + 1) * heads)
        left = jnp.concatenate([high, low, high, here], axis=0)[:, 0:positions].astype(BF16)
        right = jnp.concatenate(
            [
                per_head_high[mine],
                per_head_high[mine],
                per_head_low[mine],
                own_high[g : g + 1],
                own_low[g : g + 1],
                spare,
            ],
            axis=0,
        ).astype(BF16)
        scores = lax.dot_general(
            left, right, (((0,), (0,)), ((), ())), preferred_element_type=F32
        )
        out[g] = activation[g].astype(F32) * active[g].astype(F32) * scores
        if (g + 1) % step == 0:
            copies.append(
                pltpu.make_async_copy(
                    out.at[g + 1 - step : g + 1], out_hbm.at[g + 1 - step : g + 1], sems.at[g // step]
                )
            )
            copies[-1].start()
    for copy in copies:
        copy.wait()


def on_device(
    target_ids,
    target_pos,
    unembed,
    attn_weights,
    inv_rms,
    norm_gain,
    w_value,
    w_out,
    decoder,
    activation,
    active,
):
    vocab_rows, width = unembed.shape
    targets = target_ids.shape[0]
    columns = w_value.shape[1]
    heads = lax.axis_size(MP)
    first_row = lax.axis_index(ALL) * vocab_rows
    target = lax.axis_index(("x", "y")).reshape(1)
    block = lax.axis_index(MP).reshape(1)

    own = first_row + jnp.arange(vocab_rows, dtype=jnp.int32)
    picker = (target_ids[:, None] == own[None, :]).astype(BF16)
    found = jnp.dot(picker, unembed, preferred_element_type=F32)
    found = call(
        share_rows, shape((2 * targets, 2, width // 2), BF16), [SMEM, SMEM, VMEM], "share_rows"
    )(target, block, found)
    parts = lax.all_to_all(found, ("x", "y", "core"), 0, 0, tiled=True)
    ring = lax.axis_size(("zl", "zh"))
    parts = call(
        sum_and_repeat, shape((ring, 2, width // 2), BF16), [VMEM], "sum_and_repeat"
    )(parts)
    parts = lax.all_to_all(parts, ("zl", "zh"), 0, 0, tiled=True)
    row, asked = call(
        query_gradient,
        (shape((2, width // 2), F32), shape((heads, 8, LANES), F32)),
        [SMEM, SMEM, VMEM, VMEM, VMEM, VMEM],
        "query_gradient",
    )(target_pos, target, parts, w_out[0], attn_weights[0], inv_rms)
    heard = lax.all_to_all(asked, MP, 0, 0, tiled=True)
    blocks = call(
        lower_block,
        shape((heads, heads, columns), BF16),
        [SMEM, VMEM, VMEM, VMEM],
        "lower_block",
    )(block, heard, w_value, norm_gain)
    blocks = lax.all_to_all(blocks, MP, 0, 0, tiled=True)
    length = width + 2 * POSITIONS + columns
    message = call(
        build_message, shape((targets, heads, length), BF16), [VMEM, VMEM, VMEM], "build_message"
    )(blocks, heard, row)
    message = lax.all_to_all(message, ("x", "y"), 0, 0, tiled=True)
    return pl.pallas_call(
        score,
        out_shape=shape(activation.shape, F32),
        in_specs=[SMEM, VMEM, VMEM, VMEM, VMEM],
        out_specs=HBM,
        scratch_shapes=[pltpu.VMEM(activation.shape, F32), pltpu.SemaphoreType.DMA((4,))],
        name="score",
        compiler_params=pltpu.CompilerParams(vmem_limit_bytes=32 * 1024 * 1024),
    )(target_pos, message, decoder, activation, active)


def solution(mesh):
    mesh = Mesh(mesh.devices.reshape(4, 2, 4, 4, 4), ALL)
    in_specs = (
        P(),
        P(),
        P(ALL, None),
        P(MP, None, None, None),
        P(),
        P(),
        P(None, MP, None),
        P(MP, None, None),
        P(None, ALL, None),
        P(None, None, ALL),
        P(None, None, ALL),
    )
    out_specs = P(None, None, ALL)
    return jax.shard_map(
        on_device, mesh=mesh, in_specs=in_specs, out_specs=out_specs, check_vma=False
    )
```

```python
import jax
import jax.numpy as jnp
from jax import lax
from jax.experimental import pallas as pl
from jax.experimental.pallas import tpu as pltpu
from jax.sharding import Mesh, PartitionSpec as P

MP = ("zl", "core")
FEAT = ("x", "zh", "y")
ALL = MP + FEAT
LANES = 128
POSITIONS = 48
F32 = jnp.float32
BF16 = jnp.bfloat16
NT = (((1,), (1,)), ((), ()))
VMEM = pl.BlockSpec(memory_space=pltpu.VMEM)
SMEM = pl.BlockSpec(memory_space=pltpu.SMEM)
HBM = pl.BlockSpec(memory_space=pltpu.HBM)


def call(body, shapes, in_specs, name):
    return pl.pallas_call(
        body,
        out_shape=shapes,
        in_specs=in_specs,
        out_specs=jax.tree.map(lambda _: VMEM, shapes),
        name=name,
        compiler_params=pltpu.CompilerParams(vmem_limit_bytes=32 * 1024 * 1024),
    )


def shape(dims, kind):
    return jax.ShapeDtypeStruct(dims, kind)


def share_rows(target, block, found, out):
    del target, block
    half = out.shape[2]
    for g in range(found.shape[0]):
        row = jnp.concatenate([found[g : g + 1, :half], found[g : g + 1, half:]], axis=0)
        row = row.astype(BF16)
        out[2 * g] = row
        out[2 * g + 1] = row


def total(parts):
    value = parts[0].astype(F32)
    for i in range(1, parts.shape[0]):
        value = value + parts[i].astype(F32)
    return value


def sum_and_repeat(parts, out):
    row = total(parts).astype(BF16)
    for i in range(out.shape[0]):
        out[i] = row


def query_gradient(position, target, parts, w_out, attn, inv_rms, row_out, out):
    row = total(parts)
    row_out[...] = row
    flat = jnp.concatenate([row[0:1], row[1:2]], axis=1).astype(BF16)
    gradient = lax.dot_general(flat, w_out[...], NT, preferred_element_type=F32)
    here = position[target[0]]
    weights = attn[target[0], pl.ds(here, 1), :]
    key = lax.broadcasted_iota(jnp.int32, weights.shape, 1)
    weights = jnp.where(key <= here, weights, 0.0)
    scale = weights / jnp.sum(weights, axis=1, keepdims=True)
    scale = scale * inv_rms[pl.ds(target[0], 1), :]
    positions = weights.shape[1]
    count = gradient.shape[1] // LANES
    high = scale.astype(BF16).astype(F32)
    gap = jnp.zeros((1, LANES - positions), F32)
    lines = [gradient[:, k * LANES : (k + 1) * LANES] for k in range(count)]
    lines += [jnp.concatenate([part, gap], axis=1) for part in (high, scale - high)]
    lines.append(jnp.zeros((out.shape[1] - len(lines), LANES), F32))
    message = jnp.concatenate(lines, axis=0).astype(BF16)
    for i in range(out.shape[0]):
        out[i] = message


def lower_block(block, heard, w_value, gain, out):
    heads = heard.shape[0]
    kv_heads, columns, _ = w_value.shape
    rows = heard[...].astype(F32)
    gradient = jnp.concatenate([rows[:, 0, :], rows[:, 1, :]], axis=1).astype(BF16)
    head = lax.broadcasted_iota(jnp.int32, (heads, columns), 0)
    lowered = jnp.zeros((heads, columns), F32)
    for v in range(kv_heads):
        value = lax.dot_general(gradient, w_value[v], NT, preferred_element_type=F32)
        lowered = jnp.where(head // (heads // kv_heads) == v, value, lowered)
    whole = gain[...].reshape(1, heads * columns)
    own_gain = jnp.zeros((1, columns), F32)
    for i in range(heads):
        part = whole[:, i * columns : (i + 1) * columns]
        own_gain = jnp.where(block[0] == i, part, own_gain)
    lowered = (lowered * own_gain).astype(BF16)
    for i in range(out.shape[0]):
        out[i] = lowered


def build_message(blocks, heard, row, out):
    heads = heard.shape[0]
    members = blocks.shape[0]
    width = members * blocks.shape[2]
    lowered = jnp.concatenate([blocks[i].astype(F32) for i in range(members)], axis=1)
    lowered = lowered.astype(BF16)
    asked = heard[...].astype(F32)
    high = asked[:, 2, 0:POSITIONS]
    low = asked[:, 3, 0:POSITIONS]
    flat = jnp.concatenate([row[0:1], row[1:2]], axis=1)
    columns = width // heads
    rows = jnp.concatenate(
        [flat[:, i * columns : (i + 1) * columns] for i in range(heads)], axis=0
    )
    tail = jnp.concatenate([high, low, rows], axis=1).astype(BF16)
    for i in range(out.shape[0]):
        out[i, :, 0:width] = lowered
        out[i, :, width:] = tail


def score(position, message, decoder, activation, active, out_hbm, out, sems):
    targets, heads, _ = message.shape
    _, features, width = decoder.shape
    positions = activation.shape[1]
    columns = width // heads
    tail = message[:, :, width:].astype(F32)
    chunks = tail[:, :, 2 * positions : 2 * positions + columns]
    direction = jnp.concatenate([chunks[:, i, :] for i in range(heads)], axis=1).astype(BF16)
    lowered = message[:, :, 0:width].reshape(targets * heads, width)
    both = jnp.concatenate([lowered, direction], axis=0)
    bottom = lax.dot_general(both, decoder[0], NT, preferred_element_type=F32)
    top = lax.dot_general(decoder[1], direction, NT, preferred_element_type=F32).T
    per_head = bottom[0 : targets * heads]
    own = bottom[targets * heads :] + top
    per_head_high = per_head.astype(BF16).astype(F32)
    per_head_low = per_head - per_head_high
    own_high = own.astype(BF16).astype(F32)
    own_low = own - own_high
    scale = tail[:, :, 0:LANES]
    key = lax.broadcasted_iota(jnp.int32, (heads, LANES), 1)
    below_two = lax.broadcasted_iota(jnp.int32, (heads, LANES), 0) < 2
    spare = jnp.zeros((heads - 2, features), F32)
    step = targets // 8
    copies = []
    for g in range(targets):
        high = scale[g]
        low = pltpu.roll(high, LANES - positions, 1)
        here = jnp.where(below_two & (key == position[g]), 1.0, 0.0)
        mine = slice(g * heads, (g + 1) * heads)
        left = jnp.concatenate([high, low, high, here], axis=0)[:, 0:positions].astype(BF16)
        right = jnp.concatenate(
            [
                per_head_high[mine],
                per_head_high[mine],
                per_head_low[mine],
                own_high[g : g + 1],
                own_low[g : g + 1],
                spare,
            ],
            axis=0,
        ).astype(BF16)
        scores = lax.dot_general(
            left, right, (((0,), (0,)), ((), ())), preferred_element_type=F32
        )
        out[g] = activation[g].astype(F32) * active[g].astype(F32) * scores
        if (g + 1) % step == 0:
            copies.append(
                pltpu.make_async_copy(
                    out.at[g + 1 - step : g + 1], out_hbm.at[g + 1 - step : g + 1], sems.at[g // step]
                )
            )
            copies[-1].start()
    for copy in copies:
        copy.wait()


def on_device(
    target_ids,
    target_pos,
    unembed,
    attn_weights,
    inv_rms,
    norm_gain,
    w_value,
    w_out,
    decoder,
    activation,
    active,
):
    vocab_rows, width = unembed.shape
    targets = target_ids.shape[0]
    columns = w_value.shape[1]
    heads = lax.axis_size(MP)
    first_row = lax.axis_index(ALL) * vocab_rows
    target = lax.axis_index(("x", "y")).reshape(1)
    block = lax.axis_index(MP).reshape(1)

    own = first_row + jnp.arange(vocab_rows, dtype=jnp.int32)
    picker = (target_ids[:, None] == own[None, :]).astype(BF16)
    found = jnp.dot(picker, unembed, preferred_element_type=F32)
    found = call(
        share_rows, shape((2 * targets, 2, width // 2), BF16), [SMEM, SMEM, VMEM], "share_rows"
    )(target, block, found)
    parts = lax.all_to_all(found, ("x", "y", "core"), 0, 0, tiled=True)
    ring = lax.axis_size(("zl", "zh"))
    parts = call(
        sum_and_repeat, shape((ring, 2, width // 2), BF16), [VMEM], "sum_and_repeat"
    )(parts)
    parts = lax.all_to_all(parts, ("zl", "zh"), 0, 0, tiled=True)
    row, asked = call(
        query_gradient,
        (shape((2, width // 2), F32), shape((heads, 8, LANES), BF16)),
        [SMEM, SMEM, VMEM, VMEM, VMEM, VMEM],
        "query_gradient",
    )(target_pos, target, parts, w_out[0], attn_weights[0], inv_rms)
    heard = lax.all_to_all(asked, MP, 0, 0, tiled=True)
    blocks = call(
        lower_block,
        shape((heads, heads, columns), BF16),
        [SMEM, VMEM, VMEM, VMEM],
        "lower_block",
    )(block, heard, w_value, norm_gain)
    blocks = lax.all_to_all(blocks, MP, 0, 0, tiled=True)
    length = width + 2 * POSITIONS + columns
    message = call(
        build_message, shape((targets, heads, length), BF16), [VMEM, VMEM, VMEM], "build_message"
    )(blocks, heard, row)
    message = lax.all_to_all(message, ("x", "y"), 0, 0, tiled=True)
    return pl.pallas_call(
        score,
        out_shape=shape(activation.shape, F32),
        in_specs=[SMEM, VMEM, VMEM, VMEM, VMEM],
        out_specs=HBM,
        scratch_shapes=[pltpu.VMEM(activation.shape, F32), pltpu.SemaphoreType.DMA((8,))],
        name="score",
        compiler_params=pltpu.CompilerParams(vmem_limit_bytes=32 * 1024 * 1024),
    )(target_pos, message, decoder, activation, active)


def solution(mesh):
    mesh = Mesh(mesh.devices.reshape(4, 2, 4, 4, 4), ALL)
    in_specs = (
        P(),
        P(),
        P(ALL, None),
        P(MP, None, None, None),
        P(),
        P(),
        P(None, MP, None),
        P(MP, None, None),
        P(None, ALL, None),
        P(None, None, ALL),
        P(None, None, ALL),
    )
    out_specs = P(None, None, ALL)
    return jax.shard_map(
        on_device, mesh=mesh, in_specs=in_specs, out_specs=out_specs, check_vma=False
    )
```

```python
import jax
import jax.numpy as jnp
from jax import lax
from jax.experimental import pallas as pl
from jax.experimental.pallas import tpu as pltpu
from jax.sharding import Mesh, PartitionSpec as P

MP = ("zl", "core")
FEAT = ("x", "zh", "y")
ALL = MP + FEAT
LANES = 128
POSITIONS = 48
F32 = jnp.float32
BF16 = jnp.bfloat16
NT = (((1,), (1,)), ((), ()))
VMEM = pl.BlockSpec(memory_space=pltpu.VMEM)
SMEM = pl.BlockSpec(memory_space=pltpu.SMEM)
HBM = pl.BlockSpec(memory_space=pltpu.HBM)


def call(body, shapes, in_specs, name):
    return pl.pallas_call(
        body,
        out_shape=shapes,
        in_specs=in_specs,
        out_specs=jax.tree.map(lambda _: VMEM, shapes),
        name=name,
        compiler_params=pltpu.CompilerParams(vmem_limit_bytes=32 * 1024 * 1024),
    )


def shape(dims, kind):
    return jax.ShapeDtypeStruct(dims, kind)


def share_rows(target, block, found, out):
    del target, block
    half = out.shape[2]
    for g in range(found.shape[0]):
        row = jnp.concatenate([found[g : g + 1, :half], found[g : g + 1, half:]], axis=0)
        row = row.astype(BF16)
        out[2 * g] = row
        out[2 * g + 1] = row


def total(parts):
    value = parts[0].astype(F32)
    for i in range(1, parts.shape[0]):
        value = value + parts[i].astype(F32)
    return value


def sum_and_repeat(parts, out):
    row = total(parts).astype(BF16)
    for i in range(out.shape[0]):
        out[i] = row


def query_gradient(position, target, parts, w_out, attn, inv_rms, row_out, out):
    row = total(parts)
    row_out[...] = row
    flat = jnp.concatenate([row[0:1], row[1:2]], axis=1).astype(BF16)
    gradient = lax.dot_general(flat, w_out[...], NT, preferred_element_type=F32)
    here = position[target[0]]
    weights = attn[target[0], pl.ds(here, 1), :]
    key = lax.broadcasted_iota(jnp.int32, weights.shape, 1)
    weights = jnp.where(key <= here, weights, 0.0)
    scale = weights / jnp.sum(weights, axis=1, keepdims=True)
    scale = scale * inv_rms[pl.ds(target[0], 1), :]
    positions = weights.shape[1]
    count = gradient.shape[1] // LANES
    high = scale.astype(BF16).astype(F32)
    gap = jnp.zeros((1, LANES - positions), F32)
    lines = [gradient[:, k * LANES : (k + 1) * LANES] for k in range(count)]
    lines += [jnp.concatenate([part, gap], axis=1) for part in (high, scale - high)]
    lines.append(jnp.zeros((out.shape[1] - len(lines), LANES), F32))
    message = jnp.concatenate(lines, axis=0).astype(BF16)
    for i in range(out.shape[0]):
        out[i] = message


def lower_block(block, heard, w_value, gain, out):
    heads = heard.shape[0]
    kv_heads, columns, _ = w_value.shape
    rows = heard[...].astype(F32)
    gradient = jnp.concatenate([rows[:, 0, :], rows[:, 1, :]], axis=1).astype(BF16)
    head = lax.broadcasted_iota(jnp.int32, (heads, columns), 0)
    lowered = jnp.zeros((heads, columns), F32)
    for v in range(kv_heads):
        value = lax.dot_general(gradient, w_value[v], NT, preferred_element_type=F32)
        lowered = jnp.where(head // (heads // kv_heads) == v, value, lowered)
    whole = gain[...].reshape(1, heads * columns)
    own_gain = jnp.zeros((1, columns), F32)
    for i in range(heads):
        part = whole[:, i * columns : (i + 1) * columns]
        own_gain = jnp.where(block[0] == i, part, own_gain)
    lowered = (lowered * own_gain).astype(BF16)
    for i in range(out.shape[0]):
        out[i] = lowered


def build_message(blocks, heard, row, out):
    heads = heard.shape[0]
    members = blocks.shape[0]
    width = members * blocks.shape[2]
    lowered = jnp.concatenate([blocks[i].astype(F32) for i in range(members)], axis=1)
    lowered = lowered.astype(BF16)
    asked = heard[...].astype(F32)
    high = asked[:, 2, 0:POSITIONS]
    low = asked[:, 3, 0:POSITIONS]
    flat = jnp.concatenate([row[0:1], row[1:2]], axis=1)
    columns = width // heads
    rows = jnp.concatenate(
        [flat[:, i * columns : (i + 1) * columns] for i in range(heads)], axis=0
    )
    tail = jnp.concatenate([high, low, rows], axis=1).astype(BF16)
    for i in range(out.shape[0]):
        out[i, :, 0:width] = lowered
        out[i, :, width:] = tail


def score(position, message, decoder, activation, active, out_hbm, out, sems):
    targets, heads, _ = message.shape
    _, features, width = decoder.shape
    positions = activation.shape[1]
    columns = width // heads
    tail = message[:, :, width:].astype(F32)
    chunks = tail[:, :, 2 * positions : 2 * positions + columns]
    direction = jnp.concatenate([chunks[:, i, :] for i in range(heads)], axis=1).astype(BF16)
    lowered = message[:, :, 0:width].reshape(targets * heads, width)
    both = jnp.concatenate([lowered, direction], axis=0)
    bottom = lax.dot_general(both, decoder[0], NT, preferred_element_type=F32)
    top = lax.dot_general(decoder[1], direction, NT, preferred_element_type=F32).T
    per_head = bottom[0 : targets * heads]
    own = bottom[targets * heads :] + top
    per_head_high = per_head.astype(BF16).astype(F32)
    per_head_low = per_head - per_head_high
    own_high = own.astype(BF16).astype(F32)
    own_low = own - own_high
    scale = tail[:, :, 0:LANES]
    key = lax.broadcasted_iota(jnp.int32, (heads, LANES), 1)
    below_two = lax.broadcasted_iota(jnp.int32, (heads, LANES), 0) < 2
    spare = jnp.zeros((heads - 2, features), F32)
    step = targets // 8
    copies = []
    for g in range(targets):
        high = scale[g]
        low = pltpu.roll(high, LANES - positions, 1)
        here = jnp.where(below_two & (key == position[g]), 1.0, 0.0)
        mine = slice(g * heads, (g + 1) * heads)
        left = jnp.concatenate([high, low, high, here], axis=0)[:, 0:positions].astype(BF16)
        right = jnp.concatenate(
            [
                per_head_high[mine],
                per_head_high[mine],
                per_head_low[mine],
                own_high[g : g + 1],
                own_low[g : g + 1],
                spare,
            ],
            axis=0,
        ).astype(BF16)
        scores = lax.dot_general(
            left, right, (((0,), (0,)), ((), ())), preferred_element_type=F32
        )
        out[g] = activation[g].astype(F32) * active[g].astype(F32) * scores
        if (g + 1) % step == 0:
            copies.append(
                pltpu.make_async_copy(
                    out.at[g + 1 - step : g + 1], out_hbm.at[g + 1 - step : g + 1], sems.at[g // step]
                )
            )
            copies[-1].start()
    for copy in copies:
        copy.wait()


def on_device(
    target_ids,
    target_pos,
    unembed,
    attn_weights,
    inv_rms,
    norm_gain,
    w_value,
    w_out,
    decoder,
    activation,
    active,
):
    vocab_rows, width = unembed.shape
    targets = target_ids.shape[0]
    columns = w_value.shape[1]
    heads = lax.axis_size(MP)
    first_row = lax.axis_index(ALL) * vocab_rows
    target = lax.axis_index(("x", "y")).reshape(1)
    block = lax.axis_index(MP).reshape(1)

    own = first_row + jnp.arange(vocab_rows, dtype=jnp.int32)
    picker = (target_ids[:, None] == own[None, :]).astype(BF16)
    found = jnp.dot(picker, unembed, preferred_element_type=F32)
    found = call(
        share_rows, shape((2 * targets, 2, width // 2), BF16), [SMEM, SMEM, VMEM], "share_rows"
    )(target, block, found)
    parts = lax.all_to_all(found, ("x", "y", "core"), 0, 0, tiled=True)
    ring = lax.axis_size(("zh", "zl"))
    parts = call(
        sum_and_repeat, shape((ring, 2, width // 2), BF16), [VMEM], "sum_and_repeat"
    )(parts)
    parts = lax.all_to_all(parts, ("zh", "zl"), 0, 0, tiled=True)
    row, asked = call(
        query_gradient,
        (shape((2, width // 2), F32), shape((heads, 8, LANES), BF16)),
        [SMEM, SMEM, VMEM, VMEM, VMEM, VMEM],
        "query_gradient",
    )(target_pos, target, parts, w_out[0], attn_weights[0], inv_rms)
    heard = lax.all_to_all(asked, MP, 0, 0, tiled=True)
    blocks = call(
        lower_block,
        shape((heads, heads, columns), BF16),
        [SMEM, VMEM, VMEM, VMEM],
        "lower_block",
    )(block, heard, w_value, norm_gain)
    blocks = lax.all_to_all(blocks, MP, 0, 0, tiled=True)
    length = width + 2 * POSITIONS + columns
    message = call(
        build_message, shape((targets, heads, length), BF16), [VMEM, VMEM, VMEM], "build_message"
    )(blocks, heard, row)
    message = lax.all_to_all(message, ("x", "y"), 0, 0, tiled=True)
    return pl.pallas_call(
        score,
        out_shape=shape(activation.shape, F32),
        in_specs=[SMEM, VMEM, VMEM, VMEM, VMEM],
        out_specs=HBM,
        scratch_shapes=[pltpu.VMEM(activation.shape, F32), pltpu.SemaphoreType.DMA((8,))],
        name="score",
        compiler_params=pltpu.CompilerParams(vmem_limit_bytes=32 * 1024 * 1024),
    )(target_pos, message, decoder, activation, active)


def solution(mesh):
    mesh = Mesh(mesh.devices.reshape(4, 2, 4, 4, 4), ALL)
    in_specs = (
        P(),
        P(),
        P(ALL, None),
        P(MP, None, None, None),
        P(),
        P(),
        P(None, MP, None),
        P(MP, None, None),
        P(None, ALL, None),
        P(None, None, ALL),
        P(None, None, ALL),
    )
    out_specs = P(None, None, ALL)
    return jax.shard_map(
        on_device, mesh=mesh, in_specs=in_specs, out_specs=out_specs, check_vma=False
    )
```

```python
import jax
import jax.numpy as jnp
from jax import lax
from jax.experimental import pallas as pl
from jax.experimental.pallas import tpu as pltpu
from jax.sharding import Mesh, PartitionSpec as P

MP = ("zl", "core")
FEAT = ("x", "zh", "y")
ALL = MP + FEAT
LANES = 128
POSITIONS = 48
F32 = jnp.float32
BF16 = jnp.bfloat16
NT = (((1,), (1,)), ((), ()))
VMEM = pl.BlockSpec(memory_space=pltpu.VMEM)
SMEM = pl.BlockSpec(memory_space=pltpu.SMEM)
HBM = pl.BlockSpec(memory_space=pltpu.HBM)


def call(body, shapes, in_specs, name):
    return pl.pallas_call(
        body,
        out_shape=shapes,
        in_specs=in_specs,
        out_specs=jax.tree.map(lambda _: VMEM, shapes),
        name=name,
        compiler_params=pltpu.CompilerParams(vmem_limit_bytes=32 * 1024 * 1024),
    )


def shape(dims, kind):
    return jax.ShapeDtypeStruct(dims, kind)


def share_rows(target, block, found, out):
    del target, block
    half = out.shape[2]
    for g in range(found.shape[0]):
        row = jnp.concatenate([found[g : g + 1, :half], found[g : g + 1, half:]], axis=0)
        row = row.astype(BF16)
        out[2 * g] = row
        out[2 * g + 1] = row


def total(parts):
    value = parts[0].astype(F32)
    for i in range(1, parts.shape[0]):
        value = value + parts[i].astype(F32)
    return value


def sum_and_repeat(parts, out):
    row = total(parts).astype(BF16)
    for i in range(out.shape[0]):
        out[i] = row


def query_gradient(position, target, parts, w_out, attn, inv_rms, row_out, out):
    row = total(parts)
    row_out[...] = row
    flat = jnp.concatenate([row[0:1], row[1:2]], axis=1).astype(BF16)
    gradient = lax.dot_general(flat, w_out[...], NT, preferred_element_type=F32)
    here = position[target[0]]
    weights = attn[target[0], pl.ds(here, 1), :]
    key = lax.broadcasted_iota(jnp.int32, weights.shape, 1)
    weights = jnp.where(key <= here, weights, 0.0)
    scale = weights / jnp.sum(weights, axis=1, keepdims=True)
    scale = scale * inv_rms[pl.ds(target[0], 1), :]
    positions = weights.shape[1]
    count = gradient.shape[1] // LANES
    high = scale.astype(BF16).astype(F32)
    gap = jnp.zeros((1, LANES - positions), F32)
    lines = [gradient[:, k * LANES : (k + 1) * LANES] for k in range(count)]
    lines += [jnp.concatenate([part, gap], axis=1) for part in (high, scale - high)]
    lines.append(jnp.zeros((out.shape[1] - len(lines), LANES), F32))
    message = jnp.concatenate(lines, axis=0).astype(BF16)
    for i in range(out.shape[0]):
        out[i] = message


def lower_block(block, heard, w_value, gain, out):
    heads = heard.shape[0]
    kv_heads, columns, _ = w_value.shape
    rows = heard[...].astype(F32)
    gradient = jnp.concatenate([rows[:, 0, :], rows[:, 1, :]], axis=1).astype(BF16)
    head = lax.broadcasted_iota(jnp.int32, (heads, columns), 0)
    lowered = jnp.zeros((heads, columns), F32)
    for v in range(kv_heads):
        value = lax.dot_general(gradient, w_value[v], NT, preferred_element_type=F32)
        lowered = jnp.where(head // (heads // kv_heads) == v, value, lowered)
    whole = gain[...].reshape(1, heads * columns)
    own_gain = jnp.zeros((1, columns), F32)
    for i in range(heads):
        part = whole[:, i * columns : (i + 1) * columns]
        own_gain = jnp.where(block[0] == i, part, own_gain)
    lowered = (lowered * own_gain).astype(BF16)
    for i in range(out.shape[0]):
        out[i] = lowered


def build_message(blocks, heard, row, out):
    heads = heard.shape[0]
    members = blocks.shape[0]
    width = members * blocks.shape[2]
    lowered = jnp.concatenate([blocks[i].astype(F32) for i in range(members)], axis=1)
    lowered = lowered.astype(BF16)
    asked = heard[...].astype(F32)
    high = asked[:, 2, 0:POSITIONS]
    low = asked[:, 3, 0:POSITIONS]
    flat = jnp.concatenate([row[0:1], row[1:2]], axis=1)
    columns = width // heads
    rows = jnp.concatenate(
        [flat[:, i * columns : (i + 1) * columns] for i in range(heads)], axis=0
    )
    tail = jnp.concatenate([high, low, rows], axis=1).astype(BF16)
    for i in range(out.shape[0]):
        out[i, :, 0:width] = lowered
        out[i, :, width:] = tail


def score(position, message, decoder, activation, active, out_hbm, out, sems):
    targets, heads, _ = message.shape
    _, features, width = decoder.shape
    positions = activation.shape[1]
    columns = width // heads
    tail = message[:, :, width:].astype(F32)
    chunks = tail[:, :, 2 * positions : 2 * positions + columns]
    direction = jnp.concatenate([chunks[:, i, :] for i in range(heads)], axis=1).astype(BF16)
    lowered = message[:, :, 0:width].reshape(targets * heads, width)
    both = jnp.concatenate([lowered, direction], axis=0)
    bottom = lax.dot_general(both, decoder[0], NT, preferred_element_type=F32)
    top = lax.dot_general(decoder[1], direction, NT, preferred_element_type=F32).T
    per_head = bottom[0 : targets * heads]
    own = bottom[targets * heads :] + top
    per_head_high = per_head.astype(BF16).astype(F32)
    per_head_low = per_head - per_head_high
    own_high = own.astype(BF16).astype(F32)
    own_low = own - own_high
    scale = tail[:, :, 0:LANES]
    key = lax.broadcasted_iota(jnp.int32, (heads, LANES), 1)
    below_two = lax.broadcasted_iota(jnp.int32, (heads, LANES), 0) < 2
    spare = jnp.zeros((heads - 2, features), F32)
    step = targets // 16
    copies = []
    for g in range(targets):
        high = scale[g]
        low = pltpu.roll(high, LANES - positions, 1)
        here = jnp.where(below_two & (key == position[g]), 1.0, 0.0)
        mine = slice(g * heads, (g + 1) * heads)
        left = jnp.concatenate([high, low, high, here], axis=0)[:, 0:positions].astype(BF16)
        right = jnp.concatenate(
            [
                per_head_high[mine],
                per_head_high[mine],
                per_head_low[mine],
                own_high[g : g + 1],
                own_low[g : g + 1],
                spare,
            ],
            axis=0,
        ).astype(BF16)
        scores = lax.dot_general(
            left, right, (((0,), (0,)), ((), ())), preferred_element_type=F32
        )
        out[g] = activation[g].astype(F32) * active[g].astype(F32) * scores
        if (g + 1) % step == 0:
            copies.append(
                pltpu.make_async_copy(
                    out.at[g + 1 - step : g + 1], out_hbm.at[g + 1 - step : g + 1], sems.at[g // step]
                )
            )
            copies[-1].start()
    for copy in copies:
        copy.wait()


def on_device(
    target_ids,
    target_pos,
    unembed,
    attn_weights,
    inv_rms,
    norm_gain,
    w_value,
    w_out,
    decoder,
    activation,
    active,
):
    vocab_rows, width = unembed.shape
    targets = target_ids.shape[0]
    columns = w_value.shape[1]
    heads = lax.axis_size(MP)
    first_row = lax.axis_index(ALL) * vocab_rows
    target = lax.axis_index(("x", "y")).reshape(1)
    block = lax.axis_index(MP).reshape(1)

    own = first_row + jnp.arange(vocab_rows, dtype=jnp.int32)
    picker = (target_ids[:, None] == own[None, :]).astype(BF16)
    found = jnp.dot(picker, unembed, preferred_element_type=F32)
    found = call(
        share_rows, shape((2 * targets, 2, width // 2), BF16), [SMEM, SMEM, VMEM], "share_rows"
    )(target, block, found)
    parts = lax.all_to_all(found, ("x", "y", "core"), 0, 0, tiled=True)
    ring = lax.axis_size(("zh", "zl"))
    parts = call(
        sum_and_repeat, shape((ring, 2, width // 2), BF16), [VMEM], "sum_and_repeat"
    )(parts)
    parts = lax.all_to_all(parts, ("zh", "zl"), 0, 0, tiled=True)
    row, asked = call(
        query_gradient,
        (shape((2, width // 2), F32), shape((heads, 8, LANES), BF16)),
        [SMEM, SMEM, VMEM, VMEM, VMEM, VMEM],
        "query_gradient",
    )(target_pos, target, parts, w_out[0], attn_weights[0], inv_rms)
    heard = lax.all_to_all(asked, MP, 0, 0, tiled=True)
    blocks = call(
        lower_block,
        shape((heads, heads, columns), BF16),
        [SMEM, VMEM, VMEM, VMEM],
        "lower_block",
    )(block, heard, w_value, norm_gain)
    blocks = lax.all_to_all(blocks, MP, 0, 0, tiled=True)
    length = width + 2 * POSITIONS + columns
    message = call(
        build_message, shape((targets, heads, length), BF16), [VMEM, VMEM, VMEM], "build_message"
    )(blocks, heard, row)
    message = lax.all_to_all(message, ("x", "y"), 0, 0, tiled=True)
    return pl.pallas_call(
        score,
        out_shape=shape(activation.shape, F32),
        in_specs=[SMEM, VMEM, VMEM, VMEM, VMEM],
        out_specs=HBM,
        scratch_shapes=[pltpu.VMEM(activation.shape, F32), pltpu.SemaphoreType.DMA((16,))],
        name="score",
        compiler_params=pltpu.CompilerParams(vmem_limit_bytes=32 * 1024 * 1024),
    )(target_pos, message, decoder, activation, active)


def solution(mesh):
    mesh = Mesh(mesh.devices.reshape(4, 2, 4, 4, 4), ALL)
    in_specs = (
        P(),
        P(),
        P(ALL, None),
        P(MP, None, None, None),
        P(),
        P(),
        P(None, MP, None),
        P(MP, None, None),
        P(None, ALL, None),
        P(None, None, ALL),
        P(None, None, ALL),
    )
    out_specs = P(None, None, ALL)
    return jax.shard_map(
        on_device, mesh=mesh, in_specs=in_specs, out_specs=out_specs, check_vma=False
    )
```
